32 devices in a mesh: groups: 2 (over x), tok: 16 (over z, y, core).
Axes of the slice: x: 2, y: 2, z: 4, core: 2. Of those that a mesh axis runs over, the one named last changes fastest.
Arguments:
- tokens: bfloat16 [4096, 3072], P(('groups', 'tok')), parts along dimension 0, may hold values from -6 to 6
- routes: int32 [4096, 2], P(('groups', 'tok')), parts along dimension 0, may hold values from 0 to 7, all different within a row; in each aligned block of 128 rows (0 to 127, 128 to 255, ...) at most 40 rows name the same one
- weights: bfloat16 [32768, 3072], P(('groups', 'tok')), parts along dimension 0, may hold values from -0.109375 to 0.109375
Outputs:
- whitened: bfloat16 [32768, 3072], P(('groups', 'tok')), parts along dimension 0
The draws below stay inside these ranges and needn't reach their ends.
There are 2 independent parts, one for each index of `groups`. The reference program is written for one: setup_inputs(seed, part) draws one part's arguments, and reference() takes and returns one part's arrays. A program takes and returns all parts, laid end to end along the dimension named above; each array names one. Nothing has to cross between parts.
Inputs may be any that keep to these rules, and one draw needn't show every extreme that they name: `routes`: each token names 2 different experts. Within the tokens of one device no expert is named more than 40 times, and in every draw some expert is named exactly 40 times by the tokens of some device.
All inputs are finite; a program needn't handle non-finite values.
Results may differ from the reference program's by a relative error of at most 0.0064.
The reference program's roundings to bfloat16 on the way (of `expert_rows` and `lower`) count: a program that leaves them out, or rounds other values in their place, can miss the bound.
Values may be sent and summed in bfloat16 or wider, within the bound.
A program may use at most 256 MiB of HBM per device.

```python
import math
import jax
import jax.numpy as jnp
import numpy as np
from jax import lax

D = 3072
E = 8
TOP = 2
FF_DEV = 1024
NB = 4
TOK_DEV = 128
MOST = 40
FF = 2048
TOKENS = 2048
N_TOK = 16


def level_of(key, shape, shards, smallest, largest):
    loudness, own = 1.0, jax.random.fold_in(key, 6)
    for axis_at, parts in shards:
        draws = jnp.exp(jax.random.uniform(jax.random.fold_in(own, axis_at), (parts,), jnp.float32, smallest / len(shards), largest / len(shards)))
        loudness = loudness * jnp.repeat(draws, shape[axis_at] // parts).reshape([-1 if axis == axis_at else 1 for axis in range(len(shape))])
    return loudness


def assign_block(own_key, own, number, rows, count, top, reach, skew):
    ranking = jax.random.permutation(own_key, count)
    packed, common = shares(count, rows * top, reach, skew, True), shares(count, rows * top, reach, skew, False)
    places = jnp.arange(count)

    def named(sizes, offset_by):
        used = int((sizes > 0).sum())
        fixed = max(1, used // 4)
        shifted = fixed + (places - fixed + offset_by * (used - fixed)) % max(1, count - fixed)
        return jnp.zeros((count,), jnp.int32).at[ranking[jnp.where(places < fixed, places, shifted)]].set(jnp.asarray(sizes, jnp.int32))

    sizes = jnp.where(number % 4 == 0, named(packed, number // 4), named(common, number - number // 4 - 1))
    mixed = jax.random.permutation(jax.random.fold_in(own, 3), count)
    donor, taker = mixed[0:count // 2 * 2:2], mixed[1:count // 2 * 2:2]
    margin = jnp.minimum(sizes[donor] - 1, reach - sizes[taker]) // 2
    margin = jnp.where((donor == ranking[0]) | (taker == ranking[0]) | (sizes[taker] == 0), 0, jnp.maximum(margin, 0))
    shifted = jax.random.randint(jax.random.fold_in(own, 4), (count // 2,), 0, 1 << 20) % (margin + 1)
    sizes = sizes.at[donor].add(-shifted).at[taker].add(shifted)
    members = jnp.searchsorted(jnp.cumsum(sizes), jnp.arange(rows * top), side="right").astype(jnp.int32)
    grid = members.reshape(top, rows).T
    grid = grid[jax.random.permutation(jax.random.fold_in(own, 1), rows)]
    offset_by = jax.random.randint(jax.random.fold_in(own, 2), (rows, 1), 0, top)
    return jnp.take_along_axis(grid, (jnp.arange(top)[None, :] + offset_by) % top, axis=1)


def shares(number_of, total, most, lean, full):
    portions = [(1 << 20) // math.isqrt(standing ** lean) + 1 for standing in range(1, number_of + 1)]
    largest = most if full else min(most, max(-(-total // number_of), total * portions[0] // sum(portions)))
    least = 1 if total - largest >= number_of - 1 else 0
    given, spare = [largest] + [least] * (number_of - 1), total - largest - least * (number_of - 1)
    while spare > 0:
        free = [i for i in range(1, number_of) if given[i] < largest] or [i for i in range(1, number_of) if given[i] < most]
        mass, remaining = sum([portions[i] for i in free]), spare
        for i in free:
            addition = min(most - given[i], max(1, remaining * portions[i] // mass), spare)
            given[i] = given[i] + addition
            spare = spare - addition
    return np.array(given)


def scatter_about(rng, shape, deviation, bound, shards=(), kind=jnp.bfloat16):
    level = level_of(rng, shape, shards, -0.22, 0.18) if shards else 1.0
    entries = jax.random.normal(rng, shape, jnp.float32) * deviation * level
    return jnp.minimum(jnp.maximum(entries, -bound), bound).astype(kind)


def setup_inputs(seed: int = 0, part: int = 0) -> dict:
    key_list = jax.random.split(jax.random.key(seed), 4)
    part_splits = jax.random.split(jax.random.fold_in(key_list[3], part), 4)
    tokens = scatter_about(part_splits[0], (TOKENS, D), 1.0, 6.0, ((0, 16),))
    routes_keys = jax.random.split(jax.random.fold_in(part_splits[1], 1), TOKENS // TOK_DEV)
    routes_turns = jax.random.permutation(jax.random.fold_in(part_splits[1], 3), TOKENS // TOK_DEV)
    routes = jax.vmap(lambda own, number: assign_block(jax.random.fold_in(part_splits[1], 2), own, number, TOK_DEV, E, TOP, MOST, 2))(routes_keys, routes_turns).reshape((TOKENS, TOP))
    weights = scatter_about(part_splits[2], (E * FF, D), D ** -0.5, 0.109375, ((0, 16),))
    return {"tokens": tokens, "routes": routes, "weights": weights}


damping = 256.0

def reference(tokens, routes, weights):
    slices = N_TOK // E
    hidden = FF_DEV * slices
    cap_rows = N_TOK * MOST
    band_width = D // NB
    results = []
    for expert in range(E):
        hit_count = jnp.sum((routes == expert).astype(jnp.int32), axis=1)
        row_index = jnp.nonzero(hit_count > 0, size=cap_rows, fill_value=0)[0].astype(jnp.int32)
        valid_rows = jnp.arange(cap_rows, dtype=jnp.int32) < jnp.sum(hit_count)
        expert_rows = jnp.where(valid_rows[:, None], tokens[row_index], jnp.zeros((), tokens.dtype))
        gram_matrix = lax.dot_general(expert_rows.astype(jnp.float32), expert_rows.astype(jnp.float32), (((0,), (0,)), ((), ())), preferred_element_type=jnp.float32)
        lower_bf = jnp.zeros((D, D), jnp.bfloat16)
        for section in range(NB):
            lo_col = section * band_width
            hi_col = lo_col + band_width
            column_block = gram_matrix[lo_col:, lo_col:hi_col]
            if section > 0:
                column_block = column_block - lax.dot_general(lower_bf[lo_col:, :lo_col].astype(jnp.float32), lower_bf[lo_col:hi_col, :lo_col].astype(jnp.float32), (((1,), (1,)), ((), ())), preferred_element_type=jnp.float32)
            diag_block = column_block[:band_width] + damping * jnp.eye(band_width, dtype=jnp.float32)
            diag_factor = jnp.linalg.cholesky(diag_block)
            stacked = diag_factor
            if section + 1 < NB:
                below_rows = lax.linalg.triangular_solve(diag_factor, column_block[band_width:], left_side=False, lower=True, transpose_a=True)
                stacked = jnp.concatenate([diag_factor, below_rows], 0)
            lower_bf = lower_bf.at[lo_col:, lo_col:hi_col].set(stacked.astype(jnp.bfloat16))
        expert_weight = weights[expert * hidden:(expert + 1) * hidden]
        results.append(jnp.dot(expert_weight.astype(jnp.float32), lower_bf.astype(jnp.float32), preferred_element_type=jnp.float32).astype(jnp.bfloat16))
    return jnp.concatenate(results, 0)
```

```python
import functools

import jax
import jax.numpy as jnp
from jax import lax
from jax.experimental import pallas as pl
from jax.experimental.pallas import tpu as pltpu
from jax.sharding import PartitionSpec as P

E = 8
NB = 4
BLK = 128
TILE = 256

damping = 256.0


def partner_2(block, axis, bit):
    count = lax.axis_size(axis)
    route = []
    for low in range(count):
        high = low | 1 << bit
        if high != low and high < count:
            route += [(low, high), (high, low)]
    return lax.ppermute(block, axis, route)


def collect_rows(own_piece, slices):
    bit_count = slices.bit_length() - 1
    for bit_pos in range(bit_count):
        partner = partner_2(own_piece, "tok", bit_pos)
        own_piece = jnp.concatenate([own_piece, partner], 0)
    return own_piece


def slot_rows(target, slot_total, tokens):
    tok_rows = tokens.shape[0]
    slot_table = (target[None, :] == jnp.arange(slot_total, dtype=jnp.int32)[:, None]).astype(
        jnp.int32
    )
    slot_table = jnp.sum(slot_table.reshape(slot_total, tok_rows, 2), axis=2).astype(jnp.bfloat16)
    return jnp.dot(slot_table, tokens, preferred_element_type=jnp.float32).astype(jnp.bfloat16)


def spread(row):
    return jnp.broadcast_to(row, (8, BLK))


def inverse_factor(block_ref, inv_ref, beside):
    lane = lax.broadcasted_iota(jnp.int32, (8, BLK), 1)
    sub = lax.broadcasted_iota(jnp.int32, (8, BLK), 0)
    groups = BLK // 8
    rows = [block_ref[8 * r : 8 * r + 8, :] for r in range(groups)]
    for g in range(groups):
        first = 8 * g
        inside = (lane >= first) & (lane < first + 8)
        cols = {
            r: [spread(rows[r][:, first + j : first + j + 1]) for j in range(8)]
            for r in range(g, groups)
        }
        own = jnp.where(inside, jnp.where(lane == first + sub, 1.0, 0.0), rows[g])
        diag = list(cols[g])
        done = jnp.zeros((8, BLK), jnp.float32)
        for j in range(8):
            root = lax.rsqrt(spread(diag[j][j : j + 1, :]))
            recip = root * root
            pivot = spread(own[j : j + 1, :])
            at = sub == j
            done = jnp.where(at, pivot * root, done)
            scaled = pivot * recip
            own = jnp.where(at, scaled, own - diag[j] * scaled)
            for m in range(j + 1, 8):
                step = spread(diag[m][j : j + 1, :]) * recip
                diag[m] = jnp.where(at, step, diag[m] - diag[j] * step)
        inv_ref[first : first + 8, :] = jnp.where(lane <= first + sub, done, 0.0)
        parts = [spread(own[j : j + 1, :]) for j in range(8)]
        for r in range(g + 1, groups):
            total = jnp.where(inside, 0.0, rows[r])
            for j in range(8):
                total = total - cols[r][j] * parts[j]
            rows[r] = total
        beside(g, groups)


def split(value):
    high = value.astype(jnp.bfloat16)
    return high, (value - high.astype(jnp.float32)).astype(jnp.bfloat16)


def solve_tile(left, panel_tile, first_row, first_col):
    high, low = split(panel_tile)
    right = jnp.concatenate([high, low, high], 0)
    value = jnp.dot(left, right, preferred_element_type=jnp.float32)
    row = first_row + lax.broadcasted_iota(jnp.int32, value.shape, 0)
    col = first_col + lax.broadcasted_iota(jnp.int32, value.shape, 1)
    return jnp.where(col >= row, value, 0.0).astype(jnp.bfloat16)


def factor_kernel(x_ref, u_ref, x_t, u_t, wide, held, panel, own_t, left_ref, inv_ref, block_ref):
    features = x_ref.shape[1]
    tiles = features // TILE
    width = features // NB
    panels = width // BLK
    panel[...] = jnp.zeros_like(panel)
    left_ref[...] = jnp.zeros_like(left_ref)

    def band(k, carry):
        low = pl.multiple_of(k * width, width)

        def clear(p, c):
            held[pl.ds(pl.multiple_of(p * BLK, BLK), BLK), :] = jnp.zeros(
                (BLK, features), jnp.bfloat16
            )
            return c

        lax.fori_loop(0, panels + 1, clear, 0)

        def turn(p, c):
            at = pl.multiple_of(p * BLK, BLK)
            x_t[pl.ds(at, BLK), :] = x_ref[:, pl.ds(low + at, BLK)].T

            def turn_u(q, d):
                q_at = pl.multiple_of(q * width, width)
                u_t[pl.ds(at, BLK), pl.ds(q_at, width)] = u_ref[
                    pl.ds(q_at, width), pl.ds(low + at, BLK)
                ].T
                return d

            return lax.fori_loop(0, k, turn_u, c)

        lax.fori_loop(0, panels, turn, 0)

        def deep(t, c):
            at = pl.multiple_of(t * TILE, TILE)
            wide[:, pl.ds(at, TILE)] = jnp.dot(
                x_t[...], x_ref[:, pl.ds(at, TILE)], preferred_element_type=jnp.float32
            )

            def less(q, d):
                q_at = pl.multiple_of(q * width, width)
                wide[:, pl.ds(at, TILE)] -= jnp.dot(
                    u_t[:, pl.ds(q_at, width)],
                    u_ref[pl.ds(q_at, width), pl.ds(at, TILE)],
                    preferred_element_type=jnp.float32,
                )
                return d

            return lax.fori_loop(0, k, less, c)

        lax.fori_loop(k * (width // TILE), tiles, deep, 0)

        def step(p, c):
            r_at = pl.multiple_of(p * BLK, BLK)
            start = pl.multiple_of(low + r_at, BLK)
            left = left_ref[...]
            held[pl.ds(r_at, BLK), pl.ds(start, BLK)] = solve_tile(
                left, panel[:, pl.ds(start, BLK)], start - BLK, start
            )
            own_t[...] = held[0:width, pl.ds(start, BLK)].T
            ident = lax.broadcasted_iota(jnp.int32, (BLK, BLK), 0) == lax.broadcasted_iota(
                jnp.int32, (BLK, BLK), 1
            )
            block_ref[...] = (
                wide[pl.ds(r_at, BLK), pl.ds(start, BLK)]
                + jnp.where(ident, damping, 0.0)
                - jnp.dot(
                    own_t[...],
                    held[0:width, pl.ds(start, BLK)],
                    preferred_element_type=jnp.float32,
                )
            )

            def beside(g, groups):
                for t in range(tiles):
                    if t * groups // tiles == g:
                        cols = slice(t * TILE, (t + 1) * TILE)
                        held[pl.ds(r_at, BLK), cols] = solve_tile(
                            left, panel[:, cols], start - BLK, t * TILE
                        )
                        row = start + lax.broadcasted_iota(jnp.int32, (BLK, TILE), 0)
                        col = t * TILE + lax.broadcasted_iota(jnp.int32, (BLK, TILE), 1)
                        panel[:, cols] = (
                            wide[pl.ds(r_at, BLK), cols]
                            + jnp.where(row == col, damping, 0.0)
                            - jnp.dot(
                                own_t[...],
                                held[0:width, cols],
                                preferred_element_type=jnp.float32,
                            )
                        )

            inverse_factor(block_ref, inv_ref, beside)
            high, rest = split(inv_ref[...])
            left_ref[...] = jnp.concatenate([high, high, rest], 1)
            return c

        lax.fori_loop(0, panels, step, 0)
        left = left_ref[...]

        def last(t, c):
            at = pl.multiple_of(t * TILE, TILE)
            held[width : width + BLK, pl.ds(at, TILE)] = solve_tile(
                left, panel[:, pl.ds(at, TILE)], low + width - BLK, at
            )
            return c

        lax.fori_loop(0, tiles, last, 0)
        left_ref[...] = jnp.zeros_like(left_ref)

        def keep(p, c):
            at = pl.multiple_of(p * BLK, BLK)
            u_ref[pl.ds(low + at, BLK), :] = held[pl.ds(at + BLK, BLK), :]
            return c

        lax.fori_loop(0, panels, keep, 0)
        return carry

    lax.fori_loop(0, NB, band, 0)


def upper_factor(gathered):
    rows, features = gathered.shape
    width = features // NB
    return pl.pallas_call(
        factor_kernel,
        out_shape=jax.ShapeDtypeStruct((features, features), jnp.bfloat16),
        in_specs=[pl.BlockSpec(memory_space=pltpu.VMEM)],
        out_specs=pl.BlockSpec(memory_space=pltpu.VMEM),
        scratch_shapes=[
            pltpu.VMEM((width, rows), jnp.bfloat16),
            pltpu.VMEM((width, features - width), jnp.bfloat16),
            pltpu.VMEM((width, features), jnp.float32),
            pltpu.VMEM((width + BLK, features), jnp.bfloat16),
            pltpu.VMEM((BLK, features), jnp.float32),
            pltpu.VMEM((BLK, width), jnp.bfloat16),
            pltpu.VMEM((BLK, 3 * BLK), jnp.bfloat16),
            pltpu.VMEM((BLK, BLK), jnp.float32),
            pltpu.VMEM((BLK, BLK), jnp.float32),
        ],
        compiler_params=pltpu.CompilerParams(vmem_limit_bytes=63 << 20),
    )(gathered)


def local(tokens, routes, weights):
    tok_devices = lax.axis_size("tok")
    slices = tok_devices // E
    tok_rows = tokens.shape[0]
    features = tokens.shape[1]
    most_rows = tok_rows * 5 // 16
    picked = routes.reshape(-1)
    onehot = (picked[:, None] == jnp.arange(E, dtype=jnp.int32)[None, :]).astype(jnp.int32)
    before = jnp.cumsum(onehot, axis=0) - onehot
    ranked = jnp.sum(before * onehot, axis=1)
    slot_cap = most_rows // slices
    target = (picked * slices + ranked % slices) * slot_cap + ranked // slices
    packed = slot_rows(target, tok_devices * slot_cap, tokens)
    received = lax.all_to_all(packed, "tok", split_axis=0, concat_axis=0, tiled=True)
    gathered = collect_rows(received, slices)
    upper = upper_factor(gathered)
    band_width = features // NB
    outputs = []
    for section in range(NB):
        lo = section * band_width
        outputs.append(
            lax.dot_general(
                weights[:, lo:],
                upper[lo : lo + band_width, lo:],
                (((1,), (1,)), ((), ())),
                preferred_element_type=jnp.float32,
            ).astype(jnp.bfloat16)
        )
    return jnp.concatenate(outputs, 1)


def solution(mesh):
    return jax.shard_map(
        local,
        mesh=mesh,
        in_specs=(
            P(("groups", "tok"), None),
            P(("groups", "tok"), None),
            P(("groups", "tok"), None),
        ),
        out_specs=P(("groups", "tok"), None),
        check_vma=False,
    )
```

```python
import functools

import jax
import jax.numpy as jnp
from jax import lax
from jax.experimental import pallas as pl
from jax.experimental.pallas import tpu as pltpu
from jax.sharding import PartitionSpec as P

E = 8
NB = 4
BLK = 128
TILE = 256

damping = 256.0


def exchange_kernel(count, slices, groups, packed, out, own_sem, send, recv, pass_send, pass_recv):
    me = lax.axis_index("tok")
    barrier = pltpu.get_barrier_semaphore()
    for d in range(1, count):
        pl.semaphore_signal(
            barrier,
            inc=1,
            device_id={"tok": lax.rem(me + d, count)},
            device_id_type=pl.DeviceIdType.MESH,
        )
    pl.semaphore_wait(barrier, count - 1)
    copies = []
    for d in range(1, count):
        target = lax.rem(me + d, count)
        copies.append(
            pltpu.make_async_remote_copy(
                src_ref=packed.at[target],
                dst_ref=out.at[0, d],
                send_sem=send.at[d],
                recv_sem=recv.at[d],
                device_id={"tok": target},
                device_id_type=pl.DeviceIdType.MESH,
            )
        )
        copies[-1].start()
    own = pltpu.make_async_copy(packed.at[me], out.at[0, 0], own_sem)
    own.start()
    own.wait()
    base = me // slices * slices
    size = count // groups
    passed = []
    for q in range(groups):
        for d in range(max(1, q * size), (q + 1) * size):
            copies[d - 1].wait_recv()
        for p in range(1, slices):
            partner = base + lax.rem(me - base + p, slices)
            copy = pltpu.make_async_remote_copy(
                src_ref=out.at[0, pl.ds(q * size, size)],
                dst_ref=out.at[p, pl.ds(q * size, size)],
                send_sem=pass_send.at[p - 1, q],
                recv_sem=pass_recv.at[p - 1, q],
                device_id={"tok": partner},
                device_id_type=pl.DeviceIdType.MESH,
            )
            copy.start()
            passed.append(copy)
    for copy in copies:
        copy.wait_send()
    for copy in passed:
        copy.wait()


def exchange(packed, slices):
    count, cap, features = packed.shape
    groups = 4
    return pl.pallas_call(
        functools.partial(exchange_kernel, count, slices, groups),
        out_shape=jax.ShapeDtypeStruct((slices, count, cap, features), packed.dtype),
        in_specs=[pl.BlockSpec(memory_space=pltpu.HBM)],
        out_specs=pl.BlockSpec(memory_space=pltpu.HBM),
        scratch_shapes=[
            pltpu.SemaphoreType.DMA,
            pltpu.SemaphoreType.DMA((count,)),
            pltpu.SemaphoreType.DMA((count,)),
            pltpu.SemaphoreType.DMA((slices - 1, groups)),
            pltpu.SemaphoreType.DMA((slices - 1, groups)),
        ],
        compiler_params=pltpu.CompilerParams(collective_id=0, has_side_effects=True),
    )(packed)


def slot_rows(target, slot_total, tokens):
    tok_rows = tokens.shape[0]
    slot_table = (target[None, :] == jnp.arange(slot_total, dtype=jnp.int32)[:, None]).astype(
        jnp.int32
    )
    slot_table = jnp.sum(slot_table.reshape(slot_total, tok_rows, 2), axis=2).astype(jnp.bfloat16)
    return jnp.dot(slot_table, tokens, preferred_element_type=jnp.float32).astype(jnp.bfloat16)


def spread(row):
    return jnp.broadcast_to(row, (8, BLK))


def inverse_factor(block_ref, inv_ref, beside):
    lane = lax.broadcasted_iota(jnp.int32, (8, BLK), 1)
    sub = lax.broadcasted_iota(jnp.int32, (8, BLK), 0)
    groups = BLK // 8
    rows = [block_ref[8 * r : 8 * r + 8, :] for r in range(groups)]
    for g in range(groups):
        first = 8 * g
        inside = (lane >= first) & (lane < first + 8)
        cols = {
            r: [spread(rows[r][:, first + j : first + j + 1]) for j in range(8)]
            for r in range(g, groups)
        }
        own = jnp.where(inside, jnp.where(lane == first + sub, 1.0, 0.0), rows[g])
        diag = list(cols[g])
        done = jnp.zeros((8, BLK), jnp.float32)
        for j in range(8):
            root = lax.rsqrt(spread(diag[j][j : j + 1, :]))
            recip = root * root
            pivot = spread(own[j : j + 1, :])
            at = sub == j
            done = jnp.where(at, pivot * root, done)
            scaled = pivot * recip
            own = jnp.where(at, scaled, own - diag[j] * scaled)
            for m in range(j + 1, 8):
                step = spread(diag[m][j : j + 1, :]) * recip
                diag[m] = jnp.where(at, step, diag[m] - diag[j] * step)
        inv_ref[first : first + 8, :] = jnp.where(lane <= first + sub, done, 0.0)
        parts = [spread(own[j : j + 1, :]) for j in range(8)]
        for r in range(g + 1, groups):
            total = jnp.where(inside, 0.0, rows[r])
            for j in range(8):
                total = total - cols[r][j] * parts[j]
            rows[r] = total
        beside(g, groups)


def split(value):
    high = value.astype(jnp.bfloat16)
    return high, (value - high.astype(jnp.float32)).astype(jnp.bfloat16)


def solve_tile(left, panel_tile, first_row, first_col):
    high, low = split(panel_tile)
    right = jnp.concatenate([high, low, high], 0)
    value = jnp.dot(left, right, preferred_element_type=jnp.float32)
    row = first_row + lax.broadcasted_iota(jnp.int32, value.shape, 0)
    col = first_col + lax.broadcasted_iota(jnp.int32, value.shape, 1)
    return jnp.where(col >= row, value, 0.0).astype(jnp.bfloat16)


def factor_kernel(x_ref, u_ref, x_t, u_t, wide, held, panel, own_t, left_ref, inv_ref, block_ref):
    features = x_ref.shape[1]
    tiles = features // TILE
    width = features // NB
    panels = width // BLK
    panel[...] = jnp.zeros_like(panel)
    left_ref[...] = jnp.zeros_like(left_ref)

    def band(k, carry):
        low = pl.multiple_of(k * width, width)

        def clear(p, c):
            held[pl.ds(pl.multiple_of(p * BLK, BLK), BLK), :] = jnp.zeros(
                (BLK, features), jnp.bfloat16
            )
            return c

        lax.fori_loop(0, panels + 1, clear, 0)

        def turn(p, c):
            at = pl.multiple_of(p * BLK, BLK)
            x_t[pl.ds(at, BLK), :] = x_ref[:, pl.ds(low + at, BLK)].T

            def turn_u(q, d):
                q_at = pl.multiple_of(q * width, width)
                u_t[pl.ds(at, BLK), pl.ds(q_at, width)] = u_ref[
                    pl.ds(q_at, width), pl.ds(low + at, BLK)
                ].T
                return d

            return lax.fori_loop(0, k, turn_u, c)

        lax.fori_loop(0, panels, turn, 0)

        def deep(t, c):
            at = pl.multiple_of(t * TILE, TILE)
            wide[:, pl.ds(at, TILE)] = jnp.dot(
                x_t[...], x_ref[:, pl.ds(at, TILE)], preferred_element_type=jnp.float32
            )

            def less(q, d):
                q_at = pl.multiple_of(q * width, width)
                wide[:, pl.ds(at, TILE)] -= jnp.dot(
                    u_t[:, pl.ds(q_at, width)],
                    u_ref[pl.ds(q_at, width), pl.ds(at, TILE)],
                    preferred_element_type=jnp.float32,
                )
                return d

            return lax.fori_loop(0, k, less, c)

        lax.fori_loop(k * (width // TILE), tiles, deep, 0)

        def step(p, c):
            r_at = pl.multiple_of(p * BLK, BLK)
            start = pl.multiple_of(low + r_at, BLK)
            left = left_ref[...]
            held[pl.ds(r_at, BLK), pl.ds(start, BLK)] = solve_tile(
                left, panel[:, pl.ds(start, BLK)], start - BLK, start
            )
            own_t[...] = held[0:width, pl.ds(start, BLK)].T
            ident = lax.broadcasted_iota(jnp.int32, (BLK, BLK), 0) == lax.broadcasted_iota(
                jnp.int32, (BLK, BLK), 1
            )
            block_ref[...] = (
                wide[pl.ds(r_at, BLK), pl.ds(start, BLK)]
                + jnp.where(ident, damping, 0.0)
                - jnp.dot(
                    own_t[...],
                    held[0:width, pl.ds(start, BLK)],
                    preferred_element_type=jnp.float32,
                )
            )

            def beside(g, groups):
                for t in range(tiles):
                    if t * groups // tiles == g:
                        cols = slice(t * TILE, (t + 1) * TILE)
                        held[pl.ds(r_at, BLK), cols] = solve_tile(
                            left, panel[:, cols], start - BLK, t * TILE
                        )
                        row = start + lax.broadcasted_iota(jnp.int32, (BLK, TILE), 0)
                        col = t * TILE + lax.broadcasted_iota(jnp.int32, (BLK, TILE), 1)
                        panel[:, cols] = (
                            wide[pl.ds(r_at, BLK), cols]
                            + jnp.where(row == col, damping, 0.0)
                            - jnp.dot(
                                own_t[...],
                                held[0:width, cols],
                                preferred_element_type=jnp.float32,
                            )
                        )

            inverse_factor(block_ref, inv_ref, beside)
            high, rest = split(inv_ref[...])
            left_ref[...] = jnp.concatenate([high, high, rest], 1)
            return c

        lax.fori_loop(0, panels, step, 0)
        left = left_ref[...]

        def last(t, c):
            at = pl.multiple_of(t * TILE, TILE)
            held[width : width + BLK, pl.ds(at, TILE)] = solve_tile(
                left, panel[:, pl.ds(at, TILE)], low + width - BLK, at
            )
            return c

        lax.fori_loop(0, tiles, last, 0)
        left_ref[...] = jnp.zeros_like(left_ref)

        def keep(p, c):
            at = pl.multiple_of(p * BLK, BLK)
            u_ref[pl.ds(low + at, BLK), :] = held[pl.ds(at + BLK, BLK), :]
            return c

        lax.fori_loop(0, panels, keep, 0)
        return carry

    lax.fori_loop(0, NB, band, 0)


def upper_factor(gathered):
    rows, features = gathered.shape
    width = features // NB
    return pl.pallas_call(
        factor_kernel,
        out_shape=jax.ShapeDtypeStruct((features, features), jnp.bfloat16),
        in_specs=[pl.BlockSpec(memory_space=pltpu.VMEM)],
        out_specs=pl.BlockSpec(memory_space=pltpu.VMEM),
        scratch_shapes=[
            pltpu.VMEM((width, rows), jnp.bfloat16),
            pltpu.VMEM((width, features - width), jnp.bfloat16),
            pltpu.VMEM((width, features), jnp.float32),
            pltpu.VMEM((width + BLK, features), jnp.bfloat16),
            pltpu.VMEM((BLK, features), jnp.float32),
            pltpu.VMEM((BLK, width), jnp.bfloat16),
            pltpu.VMEM((BLK, 3 * BLK), jnp.bfloat16),
            pltpu.VMEM((BLK, BLK), jnp.float32),
            pltpu.VMEM((BLK, BLK), jnp.float32),
        ],
        compiler_params=pltpu.CompilerParams(vmem_limit_bytes=63 << 20),
    )(gathered)


def whiten_kernel(columns, w_ref, u_ref, out_ref):
    features = w_ref.shape[1]
    for t in range(features // columns):

        @pl.when(pl.program_id(1) == t)
        def _():
            out_ref[...] = lax.dot_general(
                w_ref[:, t * columns :],
                u_ref[:, t * columns :],
                (((1,), (1,)), ((), ())),
                preferred_element_type=jnp.float32,
            ).astype(jnp.bfloat16)


def whiten(weights, upper):
    hidden, features = weights.shape
    columns, block = 512, min(1024, hidden)
    return pl.pallas_call(
        functools.partial(whiten_kernel, columns),
        out_shape=jax.ShapeDtypeStruct((hidden, features), jnp.bfloat16),
        grid=(hidden // block, features // columns),
        in_specs=[
            pl.BlockSpec((block, features), lambda i, t: (i, 0)),
            pl.BlockSpec((columns, features), lambda i, t: (t, 0)),
        ],
        out_specs=pl.BlockSpec((block, columns), lambda i, t: (i, t)),
        compiler_params=pltpu.CompilerParams(vmem_limit_bytes=48 << 20),
    )(weights, upper)


def local(tokens, routes, weights):
    tok_devices = lax.axis_size("tok")
    slices = tok_devices // E
    tok_rows = tokens.shape[0]
    features = tokens.shape[1]
    most_rows = tok_rows * 5 // 16
    picked = routes.reshape(-1)
    onehot = (picked[:, None] == jnp.arange(E, dtype=jnp.int32)[None, :]).astype(jnp.int32)
    before = jnp.cumsum(onehot, axis=0) - onehot
    ranked = jnp.sum(before * onehot, axis=1)
    slot_cap = most_rows // slices
    target = (picked * slices + ranked % slices) * slot_cap + ranked // slices
    packed = slot_rows(target, tok_devices * slot_cap, tokens)
    gathered = exchange(packed.reshape(tok_devices, slot_cap, features), slices)
    gathered = gathered.reshape(tok_devices * slices * slot_cap, features)
    upper = upper_factor(gathered)
    return whiten(weights, upper)


def solution(mesh):
    return jax.shard_map(
        local,
        mesh=mesh,
        in_specs=(
            P(("groups", "tok"), None),
            P(("groups", "tok"), None),
            P(("groups", "tok"), None),
        ),
        out_specs=P(("groups", "tok"), None),
        check_vma=False,
    )
```
